256 devices in a mesh: fsdp: 16 (over y, x_lo, core), hid: 16 (over z, x_hi).
Axes of the slice: x: 4 (x_hi: 2, x_lo: 2; x = x_hi * 2 + x_lo), y: 4, z: 8, core: 2. Of those that a mesh axis runs over, the one named last changes fastest.
Arguments:
- tokens: bfloat16 [4096, 16384], P('fsdp', 'hid'), may hold values from -6 to 6
- cotangent: bfloat16 [4096, 16384], P('fsdp', 'hid'), may hold values from -6 to 6
- weights: bfloat16 [7, 128, 128, 2, 128], P(None, 'fsdp', 'hid'), may hold values from -0.375 to 0.375
- strides: int32 [7], replicated, may hold values from 0 to 6, each once
Outputs:
- output: bfloat16 [4096, 16384], P('fsdp', 'hid')
- input_grad: bfloat16 [4096, 16384], P('fsdp', 'hid')
- weight_grad: float32 [7, 128, 128, 2, 128], P(None, 'fsdp', 'hid')
The draws below stay inside these ranges and needn't reach their ends.
Inputs may be any that keep to these rules, and one draw needn't show every extreme that they name: strides is a permutation of 0 to 6, so every bit of a block index is paired once.
All inputs are finite; a program needn't handle non-finite values.
Results may differ from the reference program's by a relative error of at most 0.029.
Values may be sent and summed in bfloat16 or wider, within the bound.
No kernel may reach another device: no remote copies, remote signals or barrier semaphores. Data moves between devices by JAX's collectives and lax.ppermute only.
A program may use at most 128 MiB of HBM per device.

```python
from functools import partial
import jax
import jax.numpy as jnp
from jax import lax

BS = 128
NB = 128
NF = 7
HALF = 4
TOK_DEV = 256
W = 16384
TOKENS = 4096
N_FSDP = 16


def level_of(rng, shape, shards, smallest, top_value):
    gain, own = 1.0, jax.random.fold_in(rng, 6)
    for axis_at, shards_of in shards:
        draws = jnp.exp(jax.random.uniform(jax.random.fold_in(own, axis_at), (shards_of,), jnp.float32, smallest / len(shards), top_value / len(shards)))
        gain = gain * jnp.repeat(draws, shape[axis_at] // shards_of).reshape([-1 if axis == axis_at else 1 for axis in range(len(shape))])
    return gain


def gaussian(key, extent, spread, reach, cuts=(), held_as=jnp.bfloat16):
    array = jax.random.normal(key, extent, jnp.float32) * spread
    if len(cuts) > 0:
        array = level_of(key, extent, cuts, -0.22, 0.18) * array
    return jnp.clip(array, min=-reach, max=reach).astype(held_as)


def setup_inputs(seed: int = 0) -> dict:
    keys = jax.random.split(jax.random.key(seed), 5)
    return {
        "tokens": gaussian(keys[0], (TOKENS, W), 1.0, 6.0, ((0, 16), (1, 16))),
        "cotangent": gaussian(keys[1], (TOKENS, W), 1.0, 6.0, ((0, 16), (1, 16))),
        "weights": gaussian(keys[2], (NF, BS, NB, 2, BS), (2 * BS) ** -0.5, 0.375, ((1, 16), (2, 16))),
        "strides": jax.random.permutation(keys[3], NF).astype(jnp.int32),
    }


SQRT_HALF = 0.7071067811865476
INV_SQRT_TWO_PI = 0.3989422804014327


def gelu_value(value):
    return 0.5 * value * (1.0 + jax.scipy.special.erf(value * SQRT_HALF))


def gelu_slope(value):
    return 0.5 * (1.0 + jax.scipy.special.erf(value * SQRT_HALF)) + value * jnp.exp(-0.5 * value * value) * INV_SQRT_TWO_PI


def flip_blocks(bit, blocks):
    stride = 1 << bit
    row_count, count, width = blocks.shape
    viewed = blocks.reshape(row_count, count // (2 * stride), 2, stride, width)
    return viewed[:, :, ::-1].reshape(row_count, count, width)


def partner_of(blocks, distance):
    branches = [partial(flip_blocks, bit) for bit in range(NF)]
    return lax.switch(distance, branches, blocks)


def run_block(weights, strides, totals, pair):
    tokens_blk, cot_blk = pair
    hidden = tokens_blk.reshape(TOK_DEV, NB, BS)
    saved_in = []
    saved_partner = []
    preact = None
    for factor in range(NF):
        weight_f = weights[factor].astype(jnp.float32)
        partner = partner_of(hidden, strides[factor])
        summed = jnp.einsum("tgk,kgn->tgn", hidden.astype(jnp.float32), weight_f[:, :, 0])
        summed = summed + jnp.einsum("tgk,kgn->tgn", partner.astype(jnp.float32), weight_f[:, :, 1])
        saved_in.append(hidden)
        saved_partner.append(partner)
        if factor == HALF - 1:
            preact = summed.astype(jnp.bfloat16)
            hidden = gelu_value(preact.astype(jnp.float32)).astype(jnp.bfloat16)
        else:
            hidden = summed.astype(jnp.bfloat16)
    output = hidden.reshape(TOK_DEV, NB * BS)
    grad_blocks = cot_blk.reshape(TOK_DEV, NB, BS)
    grads = []
    for factor in reversed(range(NF)):
        weight_f = weights[factor].astype(jnp.float32)
        if factor == HALF - 1:
            grad_blocks = (grad_blocks.astype(jnp.float32) * gelu_slope(preact.astype(jnp.float32))).astype(jnp.bfloat16)
        grad32 = grad_blocks.astype(jnp.float32)
        own_term = jnp.einsum("tgk,tgn->kgn", saved_in[factor].astype(jnp.float32), grad32)
        pair_term = jnp.einsum("tgk,tgn->kgn", saved_partner[factor].astype(jnp.float32), grad32)
        grads.append(jnp.stack((own_term, pair_term), axis=2))
        direct = jnp.einsum("tgn,kgn->tgk", grad32, weight_f[:, :, 0])
        crossed = jnp.einsum("tgn,kgn->tgk", grad32, weight_f[:, :, 1]).astype(jnp.bfloat16)
        moved = partner_of(crossed, strides[factor])
        grad_blocks = (direct + moved.astype(jnp.float32)).astype(jnp.bfloat16)
    grads = jnp.stack(grads[::-1])
    return totals + grads, (output, grad_blocks.reshape(TOK_DEV, NB * BS))


def reference(tokens, cotangent, weights, strides):
    tokens_in = tokens.reshape(N_FSDP, TOK_DEV, NB * BS)
    cot_in = cotangent.reshape(N_FSDP, TOK_DEV, NB * BS)
    initial = jnp.zeros((NF, BS, NB, 2, BS), jnp.float32)
    final, (outputs, input_grads) = lax.scan(partial(run_block, weights, strides), initial, (tokens_in, cot_in))
    return outputs.reshape(TOKENS, NB * BS), input_grads.reshape(TOKENS, NB * BS), final
```

```python
from functools import partial

import jax
import jax.numpy as jnp
from jax import lax
from jax.experimental import pallas as pl
from jax.experimental.pallas import tpu as pltpu
from jax.sharding import PartitionSpec as P

HALF = 4
SQRT_HALF = 0.7071067811865476
INV_SQRT_TWO_PI = 0.3989422804014327
BF = jnp.bfloat16
F32 = jnp.float32
SLOTS = {3: 6, 4: 0, 2: 1, 5: 2, 1: 3, 6: 4, 0: 5}


def swapped(block, distance):
    count = lax.axis_size("hid")
    return lax.ppermute(block, "hid", [(low, low ^ (1 << distance)) for low in range(count)])


def move(block, distance):
    return block if distance is None else swapped(block, distance)


def exchange(pairs, local_bits, bit_count):
    remote = [None] + list(range(bit_count - local_bits))
    kinds = [jnp.maximum(stride - local_bits + 1, 0) for _, stride in pairs]
    index = kinds[0]
    for kind in kinds[1:]:
        index = index * len(remote) + kind
    plans = [[]]
    for _ in pairs:
        plans = [plan + [distance] for plan in plans for distance in remote]

    def branch(plan, *blocks):
        return tuple(move(block, distance) for block, distance in zip(blocks, plan))

    return lax.switch(index, [partial(branch, plan) for plan in plans], *[b for b, _ in pairs])


def factor_matrix(ref):
    rows = ref[:, 0, 0].astype(F32)
    own = rows[:, 0].reshape(128, 128)
    pair = rows[:, 1].reshape(128, 128)
    return jnp.concatenate((own, pair), axis=0).astype(BF)


def store_shares(grad, core, slot, mine_ref, theirs_ref):
    halves = grad.reshape(2, 8, 2, 8, 128)
    for side in range(2):
        even, odd = halves[side, :, 0], halves[side, :, 1]
        mine_ref[:, slot, 0, side] = jnp.where(core == 0, even, odd).astype(BF)
        theirs_ref[:, slot, 0, side] = jnp.where(core == 0, odd, even).astype(BF)


def weight_share(inputs, grad):
    return lax.dot_general(inputs, grad, (((0,), (0,)), ((), ())), preferred_element_type=F32)


def step_kernel(step, info, *refs):
    refs = list(refs)
    h_ref, p_ref, wf_ref = refs[:3]
    del refs[:3]
    core = info[7]
    inputs = jnp.concatenate((h_ref[...], p_ref[...]), axis=1)
    summed = jnp.dot(inputs, factor_matrix(wf_ref), preferred_element_type=F32)
    if step == 0:
        grad = refs.pop(0)[...]
    else:
        direct, moved = refs.pop(0), refs.pop(0)
        grad = (direct[...] + moved[...].astype(F32)).astype(BF)
    wb_ref = refs.pop(0)
    if step == HALF - 1:
        pre = summed.astype(BF).astype(F32)
        cdf = 0.5 * (1.0 + lax.erf(pre * SQRT_HALF))
        hidden = (pre * cdf).astype(BF)
        slope = cdf + pre * jnp.exp(-0.5 * pre * pre) * INV_SQRT_TWO_PI
        grad = (grad.astype(F32) * slope).astype(BF)
    else:
        hidden = summed.astype(BF)
    if step >= HALF:
        late_grad, early_h, early_p = refs.pop(0), refs.pop(0), refs.pop(0)
        del refs[:2]
    next_ref, direct_ref, crossed_ref = refs[:3]
    del refs[:3]
    next_ref[...] = hidden
    both = lax.dot_general(
        grad, factor_matrix(wb_ref), (((1,), (1,)), ((), ())), preferred_element_type=F32
    )
    direct_ref[...] = both[:, :128]
    crossed_ref[...] = both[:, 128:].astype(BF)
    if step in (1, 2):
        refs[0][...] = grad
    if step == HALF - 1:
        store_shares(weight_share(inputs, grad), core, 0, refs[0], refs[1])
    if step >= HALF:
        store_shares(weight_share(inputs, late_grad[...]), core, 0, refs[0], refs[1])
        early = jnp.concatenate((early_h[...], early_p[...]), axis=1)
        store_shares(weight_share(early, grad), core, 1, refs[0], refs[1])


def last_kernel(info, direct_ref, moved_ref, out_ref):
    out_ref[...] = (direct_ref[...] + moved_ref[...].astype(F32)).astype(BF)


def column(rows):
    return pl.BlockSpec((rows, 128), lambda g, info: (0, g))


def partner_column(rows, factor):
    return pl.BlockSpec((rows, 128), lambda g, info: (0, g ^ info[factor]))


def factor_block(gathered, factor):
    shape = (gathered.shape[0], 1, 1) + gathered.shape[3:]
    return pl.BlockSpec(shape, lambda g, info: (0, factor, g, 0, 0, 0))


def share_block(slots, first):
    return pl.BlockSpec((8, slots, 1, 2, 8, 128), lambda g, info: (0, first, g, 0, 0, 0))


def run_step(step, info, hidden, partner, gathered, back, extras, shares):
    rows, width = hidden.shape
    blocks = width // 128
    other = 6 - step
    args = [hidden, partner, gathered]
    specs = [column(rows), partner_column(rows, step), factor_block(gathered, step)]
    args += back
    specs += [column(rows)] if step == 0 else [column(rows), partner_column(rows, other + 1)]
    args.append(gathered)
    specs.append(factor_block(gathered, other))
    act = jax.ShapeDtypeStruct((rows, width), BF)
    outs = [act, jax.ShapeDtypeStruct((rows, width), F32), act]
    out_specs = [column(rows)] * 3
    aliases = {}
    if step in (1, 2):
        outs.append(act)
        out_specs.append(column(rows))
    if step >= HALF - 1:
        share = jax.ShapeDtypeStruct((8, 7, blocks, 2, 8, 128), BF)
        outs += [share, share]
    if step == HALF - 1:
        out_specs += [share_block(1, 6)] * 2
    if step >= HALF:
        args += extras
        specs += [column(rows), column(rows), partner_column(rows, other)]
        aliases = {len(args) + 1: 3, len(args) + 2: 4}
        args += shares
        specs += [pl.BlockSpec(memory_space=pl.ANY)] * 2
        out_specs += [share_block(2, step - HALF)] * 2
    return pl.pallas_call(
        partial(step_kernel, step),
        grid_spec=pltpu.PrefetchScalarGridSpec(
            num_scalar_prefetch=1, grid=(blocks,), in_specs=specs, out_specs=out_specs
        ),
        out_shape=outs,
        input_output_aliases=aliases,
        cost_estimate=pl.CostEstimate(flops=4 * 10**8, bytes_accessed=6 * 10**6, transcendentals=0),
        name="butterfly_step",
    )(info, *args)


def run_last(info, direct, moved):
    rows, width = direct.shape
    return pl.pallas_call(
        last_kernel,
        grid_spec=pltpu.PrefetchScalarGridSpec(
            num_scalar_prefetch=1,
            grid=(width // 128,),
            in_specs=[column(rows), partner_column(rows, 0)],
            out_specs=column(rows),
        ),
        out_shape=jax.ShapeDtypeStruct((rows, width), BF),
        name="input_grad_sum",
    )(info, direct, moved)


def shards(tokens, cotangent, weights, strides):
    factors, block_count = weights.shape[0], weights.shape[2]
    local_bits = block_count.bit_length() - 1
    fsdp = lax.axis_size("fsdp")
    swap = partial(exchange, local_bits=local_bits, bit_count=factors)
    masks = jnp.where(strides < local_bits, 1 << strides, 0)
    core = lax.axis_index("fsdp") & 1
    info = jnp.concatenate((masks, core[None])).astype(jnp.int32)
    shard = weights.transpose(0, 2, 3, 1, 4)
    gathered = lax.all_gather(shard, "fsdp", axis=0, tiled=False)

    hidden = [tokens]
    partners = [swap([(tokens, strides[0])])[0]]
    grads = {factors: cotangent}
    back, shares = [cotangent], None
    for step in range(factors):
        other = factors - 1 - step
        extras = []
        if step >= HALF:
            extras = [grads[step + 1], hidden[other], partners[other]]
        result = run_step(step, info, hidden[step], partners[step], gathered, back, extras, shares)
        hidden.append(result[0])
        direct, crossed = result[1], result[2]
        if step in (1, 2):
            grads[other + 1] = result[3]
        if step >= HALF - 1:
            shares = list(result[3:])
        if step < factors - 1:
            partner, moved = swap([(hidden[-1], strides[step + 1]), (crossed, strides[other])])
            partners.append(partner)
        else:
            (moved,) = swap([(crossed, strides[0])])
        back = [direct, moved]
    input_grad = run_last(info, *back)

    mine, theirs = shares
    arrived = lax.ppermute(theirs, "fsdp", [(i, i ^ 1) for i in range(fsdp)])
    chip_sum = (mine.astype(F32) + arrived.astype(F32)).astype(BF)
    groups = [list(range(c, fsdp, 2)) for c in range(2)]
    parts = lax.all_to_all(chip_sum, "fsdp", 0, 0, axis_index_groups=groups, tiled=False)
    total = jnp.sum(parts.astype(F32), axis=0)
    total = jnp.stack([total[SLOTS[f]] for f in range(factors)])
    weight_grad = total.transpose(0, 3, 1, 2, 4)
    return (hidden[-1], input_grad, weight_grad)


def solution(mesh):
    in_specs = (P("fsdp", "hid"), P("fsdp", "hid"), P(None, "fsdp", "hid", None, None), P())
    out_specs = (P("fsdp", "hid"), P("fsdp", "hid"), P(None, "fsdp", "hid", None, None))
    return jax.shard_map(shards, mesh=mesh, in_specs=in_specs, out_specs=out_specs, check_vma=False)
```

```python
from functools import partial

import jax
import jax.numpy as jnp
from jax import lax
from jax.experimental import pallas as pl
from jax.experimental.pallas import tpu as pltpu
from jax.sharding import PartitionSpec as P

HALF = 4
FACTORS = 7
LAST = FACTORS - 1
SQRT_HALF = 0.7071067811865476
INV_SQRT_TWO_PI = 0.3989422804014327
BF = jnp.bfloat16
F32 = jnp.float32
SLOTS = {3: 6, 4: 0, 2: 1, 5: 2, 1: 3, 6: 4, 0: 5}
ANY = pl.BlockSpec(memory_space=pl.ANY)
SMEM = pl.BlockSpec(memory_space=pltpu.SMEM)
STATE = 8


def swapped(block, kind):
    if kind == 0:
        return block
    count = lax.axis_size("hid")
    return lax.ppermute(block, "hid", [(low, low ^ (1 << (kind - 1))) for low in range(count)])


def exchange_one(block, kind, kinds):
    return lax.switch(kind, [partial(swapped, kind=k) for k in range(kinds)], block)


def pair_plans(kinds):
    return [(0, 0)] + [(lo, hi) for lo in range(kinds) for hi in range(lo + 1, kinds)]


def exchange_two(first, second, index, kinds):
    def branch(plan, a, b):
        return swapped(a, plan[0]), swapped(b, plan[1])

    return lax.switch(index, [partial(branch, plan) for plan in pair_plans(kinds)], first, second)


def lanes(g):
    return pl.ds(pl.multiple_of(g * 128, 128), 128)


def factor_matrix(ref, g):
    rows = ref[:, g].astype(F32)
    own = rows[:, 0].reshape(128, 128)
    pair = rows[:, 1].reshape(128, 128)
    return jnp.concatenate((own, pair), axis=0).astype(BF)


def store_shares(grad, core, slot, g, mine_ref, theirs_ref):
    halves = grad.reshape(2, 8, 2, 8, 128)
    for side in range(2):
        even, odd = halves[side, :, 0], halves[side, :, 1]
        mine_ref[:, slot, g, side] = jnp.where(core == 0, even, odd).astype(BF)
        theirs_ref[:, slot, g, side] = jnp.where(core == 0, odd, even).astype(BF)


def weight_share(inputs, grad):
    return lax.dot_general(inputs, grad, (((0,), (0,)), ((), ())), preferred_element_type=F32)


def step_kernel(final, *refs):
    info, at, weights, tokens, cotangent, r0, r1 = refs[:7]
    refs = refs[7 + STATE :]
    hs, ps, es, ds, c0, c1, mine, theirs = refs[:STATE]
    refs = refs[STATE:]
    out = refs[0] if final else None
    if final:
        refs = refs[1:]
    h, p, wf, wb, d, mq, e, hn, q, hj, pj, late, mine_v, theirs_v, sems = refs
    blocks = h.shape[1] // 128
    s = LAST if final else at[0]
    other = LAST - s
    mask_f, mask_b = info[s, 0], info[s, 1]
    second, second_next = info[s, 2] == 1, info[s + 1, 2] == 1
    mask_e = info[other, 0]
    core = info[0, 3]
    copy = pltpu.make_async_copy

    def choose(flag, yes, no):
        pl.when(flag)(yes)
        pl.when(jnp.logical_not(flag))(no)

    copy(weights.at[:, s], wf, sems.at[2]).start()
    if final:
        copy(hs.at[LAST - 1], h, sems.at[0]).start()
    else:
        choose(
            s == 0,
            lambda: copy(tokens, h, sems.at[0]).start(),
            lambda: copy(hs.at[jnp.maximum(s - 1, 0)], h, sems.at[0]).start(),
        )
    choose(
        second,
        lambda: copy(r1, p, sems.at[1]).start(),
        lambda: copy(r0, p, sems.at[1]).start(),
    )
    copy(weights.at[:, other], wb, sems.at[3]).start()

    def start_moved():
        copy(ds, d, sems.at[4]).start()
        choose(
            second,
            lambda: copy(r0, mq, sems.at[5]).start(),
            lambda: copy(r1, mq, sems.at[5]).start(),
        )

    if final:
        start_moved()
        copy(cotangent, late, sems.at[8]).start()
        copy(tokens, hj, sems.at[6]).start()
        copy(ps.at[0], pj, sems.at[7]).start()
    else:
        choose(s == 0, lambda: copy(cotangent, e, sems.at[4]).start(), start_moved)

        @pl.when(s >= HALF)
        def _():
            copy(es.at[LAST - 1 - s], late, sems.at[8]).start()
            copy(hs.at[other - 1], hj, sems.at[6]).start()
            copy(ps.at[other], pj, sems.at[7]).start()

    copy(tokens, h, sems.at[0]).wait()
    copy(tokens, p, sems.at[1]).wait()
    copy(weights.at[:, 0], wf, sems.at[2]).wait()
    if not final:

        @pl.when(s < HALF - 1)
        def _():
            copy(p, ps.at[s], sems.at[9]).start()

    def inputs_of(first, partner, mask, g):
        return jnp.concatenate((first[:, lanes(g)], partner[:, lanes(g ^ mask)]), axis=1)

    for g in range(blocks):
        summed = jnp.dot(
            inputs_of(h, p, mask_f, g), factor_matrix(wf, g), preferred_element_type=F32
        )
        hn[:, lanes(g)] = summed.astype(BF)

    def add_moved():
        copy(ds, d, sems.at[4]).wait()
        copy(r0, mq, sems.at[5]).wait()
        for g in range(blocks):
            e[:, lanes(g)] = (d[:, lanes(g)] + mq[:, lanes(g ^ mask_b)].astype(F32)).astype(BF)

    if final:
        add_moved()
    else:
        choose(s == 0, lambda: copy(cotangent, e, sems.at[4]).wait(), add_moved)

        @pl.when(s == HALF - 1)
        def _():
            for g in range(blocks):
                pre = hn[:, lanes(g)].astype(F32)
                cdf = 0.5 * (1.0 + lax.erf(pre * SQRT_HALF))
                hn[:, lanes(g)] = (pre * cdf).astype(BF)
                slope = cdf + pre * jnp.exp(-0.5 * pre * pre) * INV_SQRT_TWO_PI
                e[:, lanes(g)] = (e[:, lanes(g)].astype(F32) * slope).astype(BF)

    if final:
        copy(hn, out, sems.at[10]).start()
    else:
        copy(hn, hs.at[s], sems.at[10]).start()
        choose(
            second_next,
            lambda: copy(hn, c1, sems.at[11]).start(),
            lambda: copy(hn, c0, sems.at[11]).start(),
        )

        @pl.when((s == 1) | (s == 2))
        def _():
            copy(e, es.at[s - 1], sems.at[15]).start()

    copy(weights.at[:, 0], wb, sems.at[3]).wait()
    for g in range(blocks):
        both = lax.dot_general(
            e[:, lanes(g)],
            factor_matrix(wb, g),
            (((1,), (1,)), ((), ())),
            preferred_element_type=F32,
        )
        d[:, lanes(g)] = both[:, :128]
        q[:, lanes(g)] = both[:, 128:].astype(BF)
    copy(d, ds, sems.at[12]).start()
    if final:
        copy(q, c0, sems.at[13]).start()
    else:
        choose(
            second_next,
            lambda: copy(q, c0, sems.at[13]).start(),
            lambda: copy(q, c1, sems.at[13]).start(),
        )

    def share_of(first, partner, mask, grad, slot):
        for g in range(blocks):
            got = weight_share(inputs_of(first, partner, mask, g), grad[:, lanes(g)])
            store_shares(got, core, slot, g, mine_v, theirs_v)

    def two_shares():
        copy(tokens, late, sems.at[8]).wait()
        copy(tokens, hj, sems.at[6]).wait()
        copy(tokens, pj, sems.at[7]).wait()
        share_of(h, p, mask_f, late, 0)
        share_of(hj, pj, mask_e, e, 1)
        pair = pl.ds((s - HALF) * 2, 2)
        for value, held, sem in ((mine_v, mine, 16), (theirs_v, theirs, 17)):
            copy(value, held.at[:, pair], sems.at[sem]).start()
        for value, held, sem in ((mine_v, mine, 16), (theirs_v, theirs, 17)):
            copy(value, held.at[:, pair], sems.at[sem]).wait()

    def one_share():
        share_of(h, p, mask_f, e, 0)
        for value, held, sem in ((mine_v, mine, 16), (theirs_v, theirs, 17)):
            copy(value.at[:, pl.ds(0, 1)], held.at[:, pl.ds(LAST, 1)], sems.at[sem]).start()
        for value, held, sem in ((mine_v, mine, 16), (theirs_v, theirs, 17)):
            copy(value.at[:, pl.ds(0, 1)], held.at[:, pl.ds(LAST, 1)], sems.at[sem]).wait()

    if final:
        two_shares()
        copy(hn, out, sems.at[10]).wait()
    else:
        pl.when(s >= HALF)(two_shares)
        pl.when(s == HALF - 1)(one_share)
        copy(hn, hs.at[0], sems.at[10]).wait()
        copy(hn, c0, sems.at[11]).wait()

        @pl.when(s < HALF - 1)
        def _():
            copy(p, ps.at[0], sems.at[9]).wait()

        @pl.when((s == 1) | (s == 2))
        def _():
            copy(e, es.at[0], sems.at[15]).wait()

    copy(d, ds, sems.at[12]).wait()
    copy(q, c0, sems.at[13]).wait()


def run_step(final, info, at, weights, tokens, cotangent, received, state):
    rows, width = tokens.shape
    blocks = width // 128
    act = pltpu.VMEM((rows, width), BF)
    matrix = pltpu.VMEM((weights.shape[0],) + weights.shape[2:], BF)
    share = pltpu.VMEM((8, 2, blocks, 2, 8, 128), BF)
    shapes = [jax.ShapeDtypeStruct(part.shape, part.dtype) for part in state]
    if final:
        shapes.append(jax.ShapeDtypeStruct((rows, width), BF))
    first = 5 + len(received)
    return pl.pallas_call(
        partial(step_kernel, final),
        in_specs=[SMEM, SMEM] + [ANY] * (first + STATE - 2),
        out_specs=[ANY] * len(shapes),
        out_shape=shapes,
        scratch_shapes=[act, act, matrix, matrix, pltpu.VMEM((rows, width), F32)]
        + [act] * 7
        + [share, share, pltpu.SemaphoreType.DMA((18,))],
        input_output_aliases={first + i: i for i in range(STATE)},
        cost_estimate=pl.CostEstimate(flops=4 * 10**8, bytes_accessed=6 * 10**6, transcendentals=0),
        name="butterfly_step",
    )(info, at, weights, tokens, cotangent, *received, *state)


def last_kernel(info, direct_ref, moved_ref, out_ref):
    mask = info[0, 0]
    for g in range(direct_ref.shape[1] // 128):
        moved = moved_ref[:, lanes(g ^ mask)].astype(F32)
        out_ref[:, lanes(g)] = (direct_ref[:, lanes(g)] + moved).astype(BF)


def run_last(info, direct, moved):
    whole = pl.BlockSpec(memory_space=pltpu.VMEM)
    return pl.pallas_call(
        last_kernel,
        in_specs=[SMEM, whole, whole],
        out_specs=whole,
        out_shape=jax.ShapeDtypeStruct(direct.shape, BF),
        name="input_grad_sum",
    )(info, direct, moved)


def allocate(shapes):
    return pl.pallas_call(
        lambda *refs: None, out_specs=[ANY] * len(shapes), out_shape=shapes, name="buffers"
    )()


def shards(tokens, cotangent, weights, strides):
    rows, width = tokens.shape
    block_count = weights.shape[2]
    local_bits = block_count.bit_length() - 1
    fsdp = lax.axis_size("fsdp")
    kinds = 1 + FACTORS - local_bits
    kind = jnp.maximum(strides - local_bits + 1, 0)
    mask = jnp.where(strides < local_bits, 1 << strides, 0)
    core = lax.axis_index("fsdp") & 1

    forward_kind = jnp.append(kind, 0)
    backward_kind = jnp.append(0, kind[::-1])
    low = jnp.minimum(forward_kind, backward_kind)
    high = jnp.maximum(forward_kind, backward_kind)
    plans = pair_plans(kinds)
    numbers = [[0] * kinds for _ in range(kinds)]
    for number, (lo, hi) in enumerate(plans):
        numbers[lo][hi] = number
    index = jnp.asarray(numbers, jnp.int32)[low, high]
    second = (forward_kind > backward_kind).at[FACTORS].set(True)
    columns = [jnp.append(mask, 0), jnp.append(0, mask[::-1]), second, jnp.full((8,), core)]
    info = jnp.stack([c.astype(jnp.int32) for c in columns], axis=1)

    shard = weights.transpose(0, 2, 3, 1, 4)
    gathered = lax.all_gather(shard, "fsdp", axis=0, tiled=False)
    first = exchange_one(tokens, kind[0], kinds)

    act = jax.ShapeDtypeStruct((rows, width), BF)
    share = jax.ShapeDtypeStruct((8, FACTORS, block_count, 2, 8, 128), BF)
    stack = lambda count: jax.ShapeDtypeStruct((count, rows, width), BF)
    direct = jax.ShapeDtypeStruct((rows, width), F32)
    state = allocate([stack(6), stack(3), stack(2), direct, act, act, share, share])

    def body(step, carry):
        received, held = carry
        held = run_step(False, info, step[None], gathered, tokens, cotangent, received, held)
        return exchange_two(held[4], held[5], index[step + 1], kinds), tuple(held)

    received, state = lax.fori_loop(0, LAST, body, ((first, first), tuple(state)))
    at = jnp.full((1,), LAST, jnp.int32)
    result = run_step(True, info, at, gathered, tokens, cotangent, received, state)
    direct, crossed, mine, theirs, output = result[3], result[4], result[6], result[7], result[8]

    arrived = lax.ppermute(theirs, "fsdp", [(i, i ^ 1) for i in range(fsdp)])
    chip_sum = (mine.astype(F32) + arrived.astype(F32)).astype(BF)
    groups = [list(range(c, fsdp, 2)) for c in range(2)]
    parts = lax.all_to_all(chip_sum, "fsdp", 0, 0, axis_index_groups=groups, tiled=False)
    moved = exchange_one(crossed, kind[0], kinds)
    input_grad = run_last(info, direct, moved)
    total = jnp.sum(parts.astype(F32), axis=0)
    total = jnp.stack([total[SLOTS[f]] for f in range(FACTORS)])
    weight_grad = total.transpose(0, 3, 1, 2, 4)
    return (output, input_grad, weight_grad)


def solution(mesh):
    in_specs = (P("fsdp", "hid"), P("fsdp", "hid"), P(None, "fsdp", "hid", None, None), P())
    out_specs = (P("fsdp", "hid"), P("fsdp", "hid"), P(None, "fsdp", "hid", None, None))
    return jax.shard_map(shards, mesh=mesh, in_specs=in_specs, out_specs=out_specs, check_vma=False)
```

```python
from functools import partial

import jax
import jax.numpy as jnp
from jax import lax
from jax.experimental import pallas as pl
from jax.experimental.pallas import tpu as pltpu
from jax.sharding import PartitionSpec as P

HALF = 4
FACTORS = 7
LAST = FACTORS - 1
SQRT_HALF = 0.7071067811865476
INV_SQRT_TWO_PI = 0.3989422804014327
BF = jnp.bfloat16
F32 = jnp.float32
SLOTS = {3: 6, 4: 0, 2: 1, 5: 2, 1: 3, 6: 4, 0: 5}
ANY = pl.BlockSpec(memory_space=pl.ANY)
SMEM = pl.BlockSpec(memory_space=pltpu.SMEM)
STATE = 9


def swapped(block, kind):
    if kind == 0:
        return block
    count = lax.axis_size("hid")
    return lax.ppermute(block, "hid", [(low, low ^ (1 << (kind - 1))) for low in range(count)])


def exchange_one(block, kind, kinds):
    return lax.switch(kind, [partial(swapped, kind=k) for k in range(kinds)], block)


def pair_plans(kinds):
    return [(0, 0)] + [(lo, hi) for lo in range(kinds) for hi in range(lo + 1, kinds)]


def exchange_two(first, second, index, kinds):
    def branch(plan, a, b):
        return swapped(a, plan[0]), swapped(b, plan[1])

    return lax.switch(index, [partial(branch, plan) for plan in pair_plans(kinds)], first, second)


def lanes(g):
    return pl.ds(pl.multiple_of(g * 128, 128), 128)


def factor_matrix(ref, g):
    rows = ref[:, :, g].astype(F32)
    own = rows[:, :, 0].reshape(128, 128)
    pair = rows[:, :, 1].reshape(128, 128)
    return jnp.concatenate((own, pair), axis=0).astype(BF)


def store_shares(grad, core, slot, g, mine_ref, theirs_ref):
    halves = grad.reshape(2, 8, 2, 8, 128)
    for side in range(2):
        even, odd = halves[side, :, 0], halves[side, :, 1]
        mine_ref[:, slot, g, side] = jnp.where(core == 0, even, odd).astype(BF)
        theirs_ref[:, slot, g, side] = jnp.where(core == 0, odd, even).astype(BF)


def weight_share(inputs, grad):
    return lax.dot_general(inputs, grad, (((0,), (0,)), ((), ())), preferred_element_type=F32)


def when(flag, act):
    if flag is True:
        act()
    elif flag is not False:
        pl.when(flag)(act)


def choose(flag, yes, no):
    when(flag, yes)
    when((not flag) if isinstance(flag, bool) else jnp.logical_not(flag), no)


def step_kernel(opening, *refs):
    info, at, wa, wa_pair, wz, wz_pair, tokens, cotangent, r0, r1 = refs[:10]
    refs = refs[10 + STATE :]
    hs, ps, es, ds, c0, c1, mine, theirs, out = refs[:STATE]
    h, p, wf, wb, d, mq, e, hn, q, hj, pj, late, mine_v, theirs_v, sems = refs[STATE:]
    blocks = h.shape[1] // 128
    s = 0 if opening else at[0]
    is_last = False if opening else s == LAST
    is_half = False if opening else s == HALF - 1
    late_half = False if opening else s >= HALF
    other = LAST - s
    mask_f, mask_b = info[s, 0], info[s, 1]
    second, second_next = info[s, 2] == 1, info[s + 1, 2] == 1
    mask_e = info[other, 0]
    core = info[0, 3]
    copy = pltpu.make_async_copy

    def fetch(own, pair, factor, held, sem):
        copy(own.at[:, factor], held.at[:, core], sems.at[sem]).start()
        copy(pair.at[:, factor], held.at[:, 1 - core], sems.at[sem + 1]).start()

    def arrived(held, sem):
        copy(wz.at[:, 0], held.at[:, 0], sems.at[sem]).wait()
        copy(wz.at[:, 0], held.at[:, 0], sems.at[sem + 1]).wait()

    if opening:
        copy(tokens, h, sems.at[0]).start()
        fetch(wz, wz_pair, 0, wf, 2)
    else:
        copy(hs.at[s - 1], h, sems.at[0]).start()
    choose(
        second,
        lambda: copy(r1, p, sems.at[1]).start(),
        lambda: copy(r0, p, sems.at[1]).start(),
    )
    if opening:
        fetch(wz, wz_pair, 1, wb, 4)
        copy(cotangent, e, sems.at[6]).start()
    else:

        def fetch_end():
            fetch(wz, wz_pair, 1, wf, 2)
            fetch(wz, wz_pair, 0, wb, 4)

        def fetch_middle():
            fetch(wa, wa_pair, s - 1, wf, 2)
            fetch(wa, wa_pair, other - 1, wb, 4)

        choose(is_last, fetch_end, fetch_middle)
        copy(ds, d, sems.at[6]).start()
        choose(
            second,
            lambda: copy(r0, mq, sems.at[7]).start(),
            lambda: copy(r1, mq, sems.at[7]).start(),
        )

        @pl.when(s >= HALF)
        def _():
            choose(
                is_last,
                lambda: copy(cotangent, late, sems.at[8]).start(),
                lambda: copy(es.at[jnp.clip(LAST - 1 - s, 0, 1)], late, sems.at[8]).start(),
            )
            choose(
                is_last,
                lambda: copy(tokens, hj, sems.at[9]).start(),
                lambda: copy(hs.at[jnp.maximum(other - 1, 0)], hj, sems.at[9]).start(),
            )
            copy(ps.at[other], pj, sems.at[10]).start()

    copy(tokens, h, sems.at[0]).wait()
    copy(tokens, p, sems.at[1]).wait()
    when(s < HALF - 1, lambda: copy(p, ps.at[s if opening else jnp.minimum(s, 2)], sems.at[11]).start())
    arrived(wf, 2)

    def inputs_of(first, partner, mask, g):
        return jnp.concatenate((first[:, lanes(g)], partner[:, lanes(g ^ mask)]), axis=1)

    for g in range(blocks):
        summed = jnp.dot(
            inputs_of(h, p, mask_f, g), factor_matrix(wf, g), preferred_element_type=F32
        )
        hn[:, lanes(g)] = summed.astype(BF)

    if opening:
        copy(cotangent, e, sems.at[6]).wait()
    else:
        copy(ds, d, sems.at[6]).wait()
        copy(r0, mq, sems.at[7]).wait()
        for g in range(blocks):
            e[:, lanes(g)] = (d[:, lanes(g)] + mq[:, lanes(g ^ mask_b)].astype(F32)).astype(BF)

        @pl.when(s == HALF - 1)
        def _():
            for g in range(blocks):
                pre = hn[:, lanes(g)].astype(F32)
                cdf = 0.5 * (1.0 + lax.erf(pre * SQRT_HALF))
                hn[:, lanes(g)] = (pre * cdf).astype(BF)
                slope = cdf + pre * jnp.exp(-0.5 * pre * pre) * INV_SQRT_TWO_PI
                e[:, lanes(g)] = (e[:, lanes(g)].astype(F32) * slope).astype(BF)

    def send_on():
        copy(hn, hs.at[s if opening else jnp.minimum(s, LAST - 1)], sems.at[12]).start()
        choose(
            second_next,
            lambda: copy(hn, c1, sems.at[13]).start(),
            lambda: copy(hn, c0, sems.at[13]).start(),
        )

    choose(is_last, lambda: copy(hn, out, sems.at[12]).start(), send_on)
    keeps_grad = False if opening else (s == 1) | (s == 2)
    when(keeps_grad, lambda: copy(e, es.at[jnp.clip(s - 1, 0, 1)], sems.at[14]).start())

    arrived(wb, 4)
    for g in range(blocks):
        both = lax.dot_general(
            e[:, lanes(g)],
            factor_matrix(wb, g),
            (((1,), (1,)), ((), ())),
            preferred_element_type=F32,
        )
        d[:, lanes(g)] = both[:, :128]
        q[:, lanes(g)] = both[:, 128:].astype(BF)
    copy(d, ds, sems.at[15]).start()
    choose(
        second_next,
        lambda: copy(q, c0, sems.at[16]).start(),
        lambda: copy(q, c1, sems.at[16]).start(),
    )

    def share_of(first, partner, mask, grad, slot):
        for g in range(blocks):
            got = weight_share(inputs_of(first, partner, mask, g), grad[:, lanes(g)])
            store_shares(got, core, slot, g, mine_v, theirs_v)

    def store(count, first):
        held = pl.ds(0, count)
        copies = [
            copy(mine_v.at[:, held], mine.at[:, pl.ds(first, count)], sems.at[17]),
            copy(theirs_v.at[:, held], theirs.at[:, pl.ds(first, count)], sems.at[18]),
        ]
        for one in copies:
            one.start()
        for one in copies:
            one.wait()

    def two_shares():
        copy(tokens, late, sems.at[8]).wait()
        copy(tokens, hj, sems.at[9]).wait()
        copy(tokens, pj, sems.at[10]).wait()
        share_of(h, p, mask_f, late, 0)
        share_of(hj, pj, mask_e, e, 1)
        store(2, jnp.clip((s - HALF) * 2, 0, 4))

    def one_share():
        share_of(h, p, mask_f, e, 0)
        store(1, LAST)

    when(late_half, two_shares)
    when(is_half, one_share)
    copy(hn, out, sems.at[12]).wait()
    choose(is_last, lambda: None, lambda: copy(hn, c0, sems.at[13]).wait())
    when(s < HALF - 1, lambda: copy(p, ps.at[0], sems.at[11]).wait())
    when(keeps_grad, lambda: copy(e, es.at[0], sems.at[14]).wait())
    copy(d, ds, sems.at[15]).wait()
    copy(q, c0, sems.at[16]).wait()


def run_step(opening, info, at, weights, tokens, cotangent, received, state):
    rows, width = tokens.shape
    blocks = width // 128
    act = pltpu.VMEM((rows, width), BF)
    matrix = pltpu.VMEM((8, 2, blocks, 2, 8, 128), BF)
    share = pltpu.VMEM((8, 2, blocks, 2, 8, 128), BF)
    shapes = [jax.ShapeDtypeStruct(part.shape, part.dtype) for part in state]
    first = 10
    return pl.pallas_call(
        partial(step_kernel, opening),
        in_specs=[SMEM, SMEM] + [ANY] * (first + STATE - 2),
        out_specs=[ANY] * len(shapes),
        out_shape=shapes,
        scratch_shapes=[act, act, matrix, matrix, pltpu.VMEM((rows, width), F32)]
        + [act] * 7
        + [share, share, pltpu.SemaphoreType.DMA((19,))],
        input_output_aliases={first + i: i for i in range(STATE)},
        cost_estimate=pl.CostEstimate(flops=4 * 10**8, bytes_accessed=6 * 10**6, transcendentals=0),
        name="butterfly_step",
    )(info, at, *weights, tokens, cotangent, *received, *state)


def last_kernel(info, direct_ref, moved_ref, out_ref):
    mask = info[0, 0]
    for g in range(direct_ref.shape[1] // 128):
        moved = moved_ref[:, lanes(g ^ mask)].astype(F32)
        out_ref[:, lanes(g)] = (direct_ref[:, lanes(g)] + moved).astype(BF)


def run_last(info, direct, moved):
    whole = pl.BlockSpec(memory_space=pltpu.VMEM)
    return pl.pallas_call(
        last_kernel,
        in_specs=[SMEM, whole, whole],
        out_specs=whole,
        out_shape=jax.ShapeDtypeStruct(direct.shape, BF),
        name="input_grad_sum",
    )(info, direct, moved)


def allocate(shapes):
    return pl.pallas_call(
        lambda *refs: None, out_specs=[ANY] * len(shapes), out_shape=shapes, name="buffers"
    )()


def shards(tokens, cotangent, weights, strides):
    rows, width = tokens.shape
    block_count = weights.shape[2]
    local_bits = block_count.bit_length() - 1
    fsdp = lax.axis_size("fsdp")
    kinds = 1 + FACTORS - local_bits
    kind = jnp.maximum(strides - local_bits + 1, 0)
    mask = jnp.where(strides < local_bits, 1 << strides, 0)
    core = lax.axis_index("fsdp") & 1

    forward_kind = jnp.append(kind, 0)
    backward_kind = jnp.append(0, kind[::-1])
    low = jnp.minimum(forward_kind, backward_kind)
    high = jnp.maximum(forward_kind, backward_kind)
    plans = pair_plans(kinds)
    numbers = [[0] * kinds for _ in range(kinds)]
    for number, (lo, hi) in enumerate(plans):
        numbers[lo][hi] = number
    index = jnp.asarray(numbers, jnp.int32)[low, high]
    second = forward_kind > backward_kind
    second = jnp.append(second[:FACTORS], True)
    columns = [jnp.append(mask, 0), jnp.append(0, mask[::-1]), second, jnp.full((8,), core)]
    info = jnp.stack([c.astype(jnp.int32) for c in columns], axis=1)

    groups = [list(range(c, fsdp, 2)) for c in range(2)]
    across = partial(
        lax.all_to_all, axis_name="fsdp", split_axis=0, concat_axis=0, axis_index_groups=groups
    )
    twin = [(i, i ^ 1) for i in range(fsdp)]
    shard = weights.transpose(0, 2, 3, 1, 4)

    def spread(part):
        return across(jnp.broadcast_to(part[None], (fsdp // 2,) + part.shape))

    def with_pair(own):
        return own, lax.ppermute(own, "fsdp", twin)

    ends = spread(jnp.stack((shard[0], shard[LAST])))
    first = exchange_one(tokens, kind[0], kinds)
    ends, first = lax.optimization_barrier((ends, first))
    middle, ends = lax.optimization_barrier((shard[1:LAST], ends))
    middle = spread(middle)
    ends = with_pair(ends)

    act = jax.ShapeDtypeStruct((rows, width), BF)
    share = jax.ShapeDtypeStruct((8, FACTORS, block_count, 2, 8, 128), BF)
    stack = lambda count: jax.ShapeDtypeStruct((count, rows, width), BF)
    direct = jax.ShapeDtypeStruct((rows, width), F32)
    state = allocate([stack(6), stack(3), stack(2), direct, act, act, share, share, act])
    at = jnp.zeros((1,), jnp.int32)
    state = run_step(True, info, at, ends + ends, tokens, cotangent, (first, first), state)
    packed = jnp.sum(index << (4 * jnp.arange(8)), dtype=jnp.int32)

    def pair_exchange(step, held):
        return exchange_two(held[4], held[5], (packed >> (4 * step)) & 15, kinds)

    def finish(step, received, held, matrices):
        args = (info, step[None], matrices + ends, tokens, cotangent, received, held)
        return tuple(run_step(False, *args))

    received = pair_exchange(1, state)
    middle, received = lax.optimization_barrier((middle, received))
    middle = with_pair(middle)
    state = finish(jnp.int32(1), received, state, middle)

    def body(step, held):
        return finish(step, pair_exchange(step, held), held, middle)

    state = lax.fori_loop(2, FACTORS, body, state)
    direct, crossed, mine, theirs, output = state[3], state[4], state[6], state[7], state[8]

    arrived = lax.ppermute(theirs, "fsdp", twin)
    chip_sum = (mine.astype(F32) + arrived.astype(F32)).astype(BF)
    parts = across(chip_sum)
    moved = exchange_one(crossed, kind[0], kinds)
    parts, moved = lax.optimization_barrier((parts, moved))
    input_grad = run_last(info, direct, moved)
    total = jnp.sum(parts.astype(F32), axis=0)
    total = jnp.stack([total[SLOTS[f]] for f in range(FACTORS)])
    weight_grad = total.transpose(0, 3, 1, 2, 4)
    return (output, input_grad, weight_grad)


def solution(mesh):
    in_specs = (P("fsdp", "hid"), P("fsdp", "hid"), P(None, "fsdp", "hid", None, None), P())
    out_specs = (P("fsdp", "hid"), P("fsdp", "hid"), P(None, "fsdp", "hid", None, None))
    return jax.shard_map(shards, mesh=mesh, in_specs=in_specs, out_specs=out_specs, check_vma=False)
```

```python
from functools import partial

import jax
import jax.numpy as jnp
from jax import lax
from jax.experimental import pallas as pl
from jax.experimental.pallas import tpu as pltpu
from jax.sharding import PartitionSpec as P

HALF = 4
FACTORS = 7
LAST = FACTORS - 1
SQRT_HALF = 0.7071067811865476
INV_SQRT_TWO_PI = 0.3989422804014327
BF = jnp.bfloat16
F32 = jnp.float32
SLOTS = {3: 6, 4: 0, 2: 1, 5: 2, 1: 3, 6: 4, 0: 5}
ANY = pl.BlockSpec(memory_space=pl.ANY)
SMEM = pl.BlockSpec(memory_space=pltpu.SMEM)
STATE = 9


def swapped(block, kind):
    if kind == 0:
        return block
    count = lax.axis_size("hid")
    return lax.ppermute(block, "hid", [(low, low ^ (1 << (kind - 1))) for low in range(count)])


def exchange_one(block, kind, kinds):
    return lax.switch(kind, [partial(swapped, kind=k) for k in range(kinds)], block)


def pair_plans(kinds):
    return [(0, 0)] + [(lo, hi) for lo in range(kinds) for hi in range(lo + 1, kinds)]


def exchange_two(first, second, index, kinds):
    def branch(plan, a, b):
        return swapped(a, plan[0]), swapped(b, plan[1])

    return lax.switch(index, [partial(branch, plan) for plan in pair_plans(kinds)], first, second)


def lanes(g):
    return pl.ds(pl.multiple_of(g * 128, 128), 128)


def factor_matrix(ref, g):
    rows = ref[:, :, g].astype(F32)
    own = rows[:, :, 0].reshape(128, 128)
    pair = rows[:, :, 1].reshape(128, 128)
    return jnp.concatenate((own, pair), axis=0).astype(BF)


def store_shares(grad, core, slot, g, mine_ref, theirs_ref):
    halves = grad.reshape(2, 8, 2, 8, 128)
    for side in range(2):
        even, odd = halves[side, :, 0], halves[side, :, 1]
        mine_ref[:, slot, g, side] = jnp.where(core == 0, even, odd).astype(BF)
        theirs_ref[:, slot, g, side] = jnp.where(core == 0, odd, even).astype(BF)


def weight_share(inputs, grad):
    return lax.dot_general(inputs, grad, (((0,), (0,)), ((), ())), preferred_element_type=F32)


def when(flag, act):
    if flag is True:
        act()
    elif flag is not False:
        pl.when(flag)(act)


def choose(flag, yes, no):
    when(flag, yes)
    when((not flag) if isinstance(flag, bool) else jnp.logical_not(flag), no)


def step_kernel(opening, *refs):
    info, at, wa, wa_pair, wz, wz_pair, tokens, cotangent, r0, r1 = refs[:10]
    refs = refs[10 + STATE :]
    hs, ps, es, ds, c0, c1, mine, theirs, out = refs[:STATE]
    h, p, wf, wb, d, mq, e, hn, q, hj, pj, late, mine_v, theirs_v, sems = refs[STATE:]
    blocks = h.shape[1] // 128
    s = 0 if opening else at[0]
    is_last = False if opening else s == LAST
    is_half = False if opening else s == HALF - 1
    late_half = False if opening else s >= HALF
    other = LAST - s
    mask_f, mask_b = info[s, 0], info[s, 1]
    second, second_next = info[s, 2] == 1, info[s + 1, 2] == 1
    mask_e = info[other, 0]
    core = info[0, 3]
    copy = pltpu.make_async_copy

    def fetch(own, pair, factor, held, sem):
        copy(own.at[:, factor], held.at[:, core], sems.at[sem]).start()
        copy(pair.at[:, factor], held.at[:, 1 - core], sems.at[sem + 1]).start()

    def arrived(held, sem):
        copy(wz.at[:, 0], held.at[:, 0], sems.at[sem]).wait()
        copy(wz.at[:, 0], held.at[:, 0], sems.at[sem + 1]).wait()

    if opening:
        copy(tokens, h, sems.at[0]).start()
        fetch(wz, wz_pair, 0, wf, 2)
    else:
        choose(
            second,
            lambda: copy(c1, h, sems.at[0]).start(),
            lambda: copy(c0, h, sems.at[0]).start(),
        )
    choose(
        second,
        lambda: copy(r1, p, sems.at[1]).start(),
        lambda: copy(r0, p, sems.at[1]).start(),
    )
    if opening:
        fetch(wz, wz_pair, 1, wb, 4)
        copy(cotangent, e, sems.at[6]).start()
    else:

        def fetch_end():
            fetch(wz, wz_pair, 1, wf, 2)
            fetch(wz, wz_pair, 0, wb, 4)

        def fetch_middle():
            fetch(wa, wa_pair, s - 1, wf, 2)
            fetch(wa, wa_pair, other - 1, wb, 4)

        choose(is_last, fetch_end, fetch_middle)
        copy(ds, d, sems.at[6]).start()
        choose(
            second,
            lambda: copy(r0, mq, sems.at[7]).start(),
            lambda: copy(r1, mq, sems.at[7]).start(),
        )

        @pl.when(s >= HALF)
        def _():
            choose(
                is_last,
                lambda: copy(cotangent, late, sems.at[8]).start(),
                lambda: copy(es.at[jnp.clip(LAST - 1 - s, 0, 1)], late, sems.at[8]).start(),
            )
            choose(
                is_last,
                lambda: copy(tokens, hj, sems.at[9]).start(),
                lambda: copy(hs.at[jnp.clip(other - 1, 0, 1)], hj, sems.at[9]).start(),
            )
            copy(ps.at[other], pj, sems.at[10]).start()

    copy(tokens, h, sems.at[0]).wait()
    copy(tokens, p, sems.at[1]).wait()
    when(s < HALF - 1, lambda: copy(p, ps.at[s if opening else jnp.minimum(s, 2)], sems.at[11]).start())
    arrived(wf, 2)

    def inputs_of(first, partner, mask, g):
        return jnp.concatenate((first[:, lanes(g)], partner[:, lanes(g ^ mask)]), axis=1)

    for g in range(blocks):
        summed = jnp.dot(
            inputs_of(h, p, mask_f, g), factor_matrix(wf, g), preferred_element_type=F32
        )
        hn[:, lanes(g)] = summed.astype(BF)

    if opening:
        copy(cotangent, e, sems.at[6]).wait()
    else:
        copy(ds, d, sems.at[6]).wait()
        copy(r0, mq, sems.at[7]).wait()
        for g in range(blocks):
            moved = mq[:, lanes(g ^ mask_b)].astype(F32)
            e[:, lanes(g)] = (d[:, lanes(g)].astype(F32) + moved).astype(BF)

        @pl.when(s == HALF - 1)
        def _():
            for g in range(blocks):
                pre = hn[:, lanes(g)].astype(F32)
                cdf = 0.5 * (1.0 + lax.erf(pre * SQRT_HALF))
                hn[:, lanes(g)] = (pre * cdf).astype(BF)
                slope = cdf + pre * jnp.exp(-0.5 * pre * pre) * INV_SQRT_TWO_PI
                e[:, lanes(g)] = (e[:, lanes(g)].astype(F32) * slope).astype(BF)

    def send_on():
        when(
            s < 2, lambda: copy(hn, hs.at[jnp.minimum(s, 1)], sems.at[12]).start()
        )
        choose(
            second_next,
            lambda: copy(hn, c1, sems.at[13]).start(),
            lambda: copy(hn, c0, sems.at[13]).start(),
        )

    choose(is_last, lambda: copy(hn, out, sems.at[12]).start(), send_on)
    keeps_grad = False if opening else (s == 1) | (s == 2)
    when(keeps_grad, lambda: copy(e, es.at[jnp.clip(s - 1, 0, 1)], sems.at[14]).start())

    arrived(wb, 4)
    for g in range(blocks):
        both = lax.dot_general(
            e[:, lanes(g)],
            factor_matrix(wb, g),
            (((1,), (1,)), ((), ())),
            preferred_element_type=F32,
        )
        d[:, lanes(g)] = both[:, :128].astype(BF)
        q[:, lanes(g)] = both[:, 128:].astype(BF)
    copy(d, ds, sems.at[15]).start()
    choose(
        second_next,
        lambda: copy(q, c0, sems.at[16]).start(),
        lambda: copy(q, c1, sems.at[16]).start(),
    )

    def share_of(first, partner, mask, grad, slot):
        for g in range(blocks):
            got = weight_share(inputs_of(first, partner, mask, g), grad[:, lanes(g)])
            store_shares(got, core, slot, g, mine_v, theirs_v)

    def store(count, first):
        held = pl.ds(0, count)
        copies = [
            copy(mine_v.at[:, held], mine.at[:, pl.ds(first, count)], sems.at[17]),
            copy(theirs_v.at[:, held], theirs.at[:, pl.ds(first, count)], sems.at[18]),
        ]
        for one in copies:
            one.start()
        for one in copies:
            one.wait()

    def two_shares():
        copy(tokens, late, sems.at[8]).wait()
        copy(tokens, hj, sems.at[9]).wait()
        copy(tokens, pj, sems.at[10]).wait()
        share_of(h, p, mask_f, late, 0)
        share_of(hj, pj, mask_e, e, 1)
        store(2, jnp.clip((s - HALF) * 2, 0, 4))

    def one_share():
        share_of(h, p, mask_f, e, 0)
        store(1, LAST)

    when(late_half, two_shares)
    when(is_half, one_share)
    when((s < 2) | is_last, lambda: copy(hn, out, sems.at[12]).wait())
    choose(is_last, lambda: None, lambda: copy(hn, c0, sems.at[13]).wait())
    when(s < HALF - 1, lambda: copy(p, ps.at[0], sems.at[11]).wait())
    when(keeps_grad, lambda: copy(e, es.at[0], sems.at[14]).wait())
    copy(d, ds, sems.at[15]).wait()
    copy(q, c0, sems.at[16]).wait()


def run_step(opening, info, at, weights, tokens, cotangent, received, state):
    rows, width = tokens.shape
    blocks = width // 128
    act = pltpu.VMEM((rows, width), BF)
    matrix = pltpu.VMEM((8, 2, blocks, 2, 8, 128), BF)
    share = pltpu.VMEM((8, 2, blocks, 2, 8, 128), BF)
    shapes = [jax.ShapeDtypeStruct(part.shape, part.dtype) for part in state]
    first = 10
    return pl.pallas_call(
        partial(step_kernel, opening),
        in_specs=[SMEM, SMEM] + [ANY] * (first + STATE - 2),
        out_specs=[ANY] * len(shapes),
        out_shape=shapes,
        scratch_shapes=[act, act, matrix, matrix, act]
        + [act] * 7
        + [share, share, pltpu.SemaphoreType.DMA((19,))],
        input_output_aliases={first + i: i for i in range(STATE)},
        cost_estimate=pl.CostEstimate(flops=4 * 10**8, bytes_accessed=6 * 10**6, transcendentals=0),
        name="butterfly_step",
    )(info, at, *weights, tokens, cotangent, *received, *state)


def last_kernel(info, direct_ref, moved_ref, out_ref):
    mask = info[0, 0]
    for g in range(direct_ref.shape[1] // 128):
        moved = moved_ref[:, lanes(g ^ mask)].astype(F32)
        out_ref[:, lanes(g)] = (direct_ref[:, lanes(g)].astype(F32) + moved).astype(BF)


def run_last(info, direct, moved):
    whole = pl.BlockSpec(memory_space=pltpu.VMEM)
    return pl.pallas_call(
        last_kernel,
        in_specs=[SMEM, whole, whole],
        out_specs=whole,
        out_shape=jax.ShapeDtypeStruct(direct.shape, direct.dtype),
        name="input_grad_sum",
    )(info, direct, moved)


def allocate(shapes):
    return pl.pallas_call(
        lambda *refs: None, out_specs=[ANY] * len(shapes), out_shape=shapes, name="buffers"
    )()


def shards(tokens, cotangent, weights, strides):
    rows, width = tokens.shape
    block_count = weights.shape[2]
    local_bits = block_count.bit_length() - 1
    fsdp = lax.axis_size("fsdp")
    kinds = 1 + FACTORS - local_bits
    kind = jnp.maximum(strides - local_bits + 1, 0)
    mask = jnp.where(strides < local_bits, 1 << strides, 0)
    core = lax.axis_index("fsdp") & 1

    forward_kind = jnp.append(kind, 0)
    backward_kind = jnp.append(0, kind[::-1])
    low = jnp.minimum(forward_kind, backward_kind)
    high = jnp.maximum(forward_kind, backward_kind)
    plans = pair_plans(kinds)
    numbers = [[0] * kinds for _ in range(kinds)]
    for number, (lo, hi) in enumerate(plans):
        numbers[lo][hi] = number
    index = jnp.asarray(numbers, jnp.int32)[low, high]
    second = forward_kind > backward_kind
    second = jnp.append(second[:FACTORS], True)
    columns = [jnp.append(mask, 0), jnp.append(0, mask[::-1]), second, jnp.full((8,), core)]
    info = jnp.stack([c.astype(jnp.int32) for c in columns], axis=1)

    groups = [list(range(c, fsdp, 2)) for c in range(2)]
    across = partial(
        lax.all_to_all, axis_name="fsdp", split_axis=0, concat_axis=0, axis_index_groups=groups
    )
    twin = [(i, i ^ 1) for i in range(fsdp)]
    shard = weights.transpose(0, 2, 3, 1, 4)

    def copies(part):
        return jnp.broadcast_to(part[None], (fsdp // 2,) + part.shape)

    def with_pair(own):
        return own, lax.ppermute(own, "fsdp", twin)

    ends = across(copies(jnp.stack((shard[0], shard[LAST]))))
    middle = copies(shard[1:LAST])
    first = exchange_one(tokens, kind[0], kinds)
    ends, first = lax.optimization_barrier((ends, first))
    middle, ends = lax.optimization_barrier((middle, ends))
    middle = across(middle)
    ends = with_pair(ends)

    act = jax.ShapeDtypeStruct((rows, width), BF)
    share = jax.ShapeDtypeStruct((8, FACTORS, block_count, 2, 8, 128), BF)
    stack = lambda count: jax.ShapeDtypeStruct((count, rows, width), BF)
    state = allocate([stack(2), stack(3), stack(2), act, act, act, share, share, act])
    at = jnp.zeros((1,), jnp.int32)
    state = run_step(True, info, at, ends + ends, tokens, cotangent, (first, first), state)
    packed = jnp.sum(index << (4 * jnp.arange(8)), dtype=jnp.int32)

    def pair_exchange(step, held):
        return exchange_two(held[4], held[5], (packed >> (4 * step)) & 15, kinds)

    def finish(step, received, held, matrices):
        args = (info, step[None], matrices + ends, tokens, cotangent, received, held)
        return tuple(run_step(False, *args))

    received = pair_exchange(1, state)
    middle, received = lax.optimization_barrier((middle, received))
    middle = with_pair(middle)
    state = finish(jnp.int32(1), received, state, middle)

    def body(step, held):
        return finish(step, pair_exchange(step, held), held, middle)

    state = lax.fori_loop(2, FACTORS, body, state)
    direct, crossed, mine, theirs, output = state[3], state[4], state[6], state[7], state[8]

    arrived = lax.ppermute(theirs, "fsdp", twin)
    chip_sum = (mine.astype(F32) + arrived.astype(F32)).astype(BF)
    parts = across(chip_sum)
    moved = exchange_one(crossed, kind[0], kinds)
    parts, _ = lax.optimization_barrier((parts, moved))
    input_grad = run_last(info, direct, moved)
    total = jnp.sum(parts.astype(F32), axis=0)
    total = jnp.stack([total[SLOTS[f]] for f in range(FACTORS)])
    weight_grad = total.transpose(0, 3, 1, 2, 4)
    return (output, input_grad, weight_grad)


def solution(mesh):
    in_specs = (P("fsdp", "hid"), P("fsdp", "hid"), P(None, "fsdp", "hid", None, None), P())
    out_specs = (P("fsdp", "hid"), P("fsdp", "hid"), P(None, "fsdp", "hid", None, None))
    return jax.shard_map(shards, mesh=mesh, in_specs=in_specs, out_specs=out_specs, check_vma=False)
```

```python
from functools import partial

import jax
import jax.numpy as jnp
from jax import lax
from jax.experimental import pallas as pl
from jax.experimental.pallas import tpu as pltpu
from jax.sharding import PartitionSpec as P

HALF = 4
FACTORS = 7
LAST = FACTORS - 1
SQRT_HALF = 0.7071067811865476
INV_SQRT_TWO_PI = 0.3989422804014327
BF = jnp.bfloat16
F32 = jnp.float32
SLOTS = {3: 6, 4: 0, 2: 1, 5: 2, 1: 3, 6: 4, 0: 5}
ANY = pl.BlockSpec(memory_space=pl.ANY)
SMEM = pl.BlockSpec(memory_space=pltpu.SMEM)
STATE = 9


def swapped(block, kind):
    if kind == 0:
        return block
    count = lax.axis_size("hid")
    distance = kind % (count.bit_length() - 1)
    return lax.ppermute(block, "hid", [(low, low ^ (1 << distance)) for low in range(count)])


def exchange_one(block, kind, kinds):
    return lax.switch(kind, [partial(swapped, kind=k) for k in range(kinds)], block)


def pair_plans(kinds):
    return [(0, 0)] + [(lo, hi) for lo in range(kinds) for hi in range(lo + 1, kinds)]


def exchange_two(first, second, index, kinds):
    def branch(plan, a, b):
        return swapped(a, plan[0]), swapped(b, plan[1])

    return lax.switch(index, [partial(branch, plan) for plan in pair_plans(kinds)], first, second)


def lanes(g):
    return pl.ds(pl.multiple_of(g * 128, 128), 128)


def factor_matrix(ref, g):
    rows = ref[:, :, g].astype(F32)
    own = rows[:, :, 0].reshape(128, 128)
    pair = rows[:, :, 1].reshape(128, 128)
    return jnp.concatenate((own, pair), axis=0).astype(BF)


def store_shares(grad, core, slot, g, mine_ref, theirs_ref):
    halves = grad.reshape(2, 8, 2, 8, 128)
    for side in range(2):
        even, odd = halves[side, :, 0], halves[side, :, 1]
        mine_ref[:, slot, g, side] = jnp.where(core == 0, even, odd).astype(BF)
        theirs_ref[:, slot, g, side] = jnp.where(core == 0, odd, even).astype(BF)


def weight_share(inputs, grad):
    return lax.dot_general(inputs, grad, (((0,), (0,)), ((), ())), preferred_element_type=F32)


def when(flag, act):
    if flag is True:
        act()
    elif flag is not False:
        pl.when(flag)(act)


def choose(flag, yes, no):
    when(flag, yes)
    when((not flag) if isinstance(flag, bool) else jnp.logical_not(flag), no)


def step_kernel(opening, *refs):
    info, at, wa, wa_pair, wz, wz_pair, tokens, cotangent, r0, r1 = refs[:10]
    refs = refs[10 + STATE :]
    hs, ps, es, ds, c0, c1, mine, theirs, out = refs[:STATE]
    h, p, wf, wb, d, mq, e, hn, q, hj, pj, late, mine_v, theirs_v, sems = refs[STATE:]
    blocks = h.shape[1] // 128
    s = 0 if opening else at[0]
    is_last = False if opening else s == LAST
    is_half = False if opening else s == HALF - 1
    late_half = False if opening else s >= HALF
    other = LAST - s
    mask_f, mask_b = info[s, 0], info[s, 1]
    second, second_next = info[s, 2] == 1, info[s + 1, 2] == 1
    mask_e = info[other, 0]
    core = info[0, 3]
    copy = pltpu.make_async_copy

    def fetch(own, pair, factor, held, sem):
        copy(own.at[:, factor], held.at[:, core], sems.at[sem]).start()
        copy(pair.at[:, factor], held.at[:, 1 - core], sems.at[sem + 1]).start()

    def arrived(held, sem):
        copy(wz.at[:, 0], held.at[:, 0], sems.at[sem]).wait()
        copy(wz.at[:, 0], held.at[:, 0], sems.at[sem + 1]).wait()

    if opening:
        copy(tokens, h, sems.at[0]).start()
        fetch(wz, wz_pair, 0, wf, 2)
    else:
        choose(
            second,
            lambda: copy(c1, h, sems.at[0]).start(),
            lambda: copy(c0, h, sems.at[0]).start(),
        )
    choose(
        second,
        lambda: copy(r1, p, sems.at[1]).start(),
        lambda: copy(r0, p, sems.at[1]).start(),
    )
    if opening:
        fetch(wz, wz_pair, 1, wb, 4)
        copy(cotangent, e, sems.at[6]).start()
    else:

        def fetch_end():
            fetch(wz, wz_pair, 1, wf, 2)
            fetch(wz, wz_pair, 0, wb, 4)

        def fetch_middle():
            fetch(wa, wa_pair, s - 1, wf, 2)
            fetch(wa, wa_pair, other - 1, wb, 4)

        choose(is_last, fetch_end, fetch_middle)
        copy(ds, d, sems.at[6]).start()
        choose(
            second,
            lambda: copy(r0, mq, sems.at[7]).start(),
            lambda: copy(r1, mq, sems.at[7]).start(),
        )

        @pl.when(s >= HALF)
        def _():
            choose(
                is_last,
                lambda: copy(cotangent, late, sems.at[8]).start(),
                lambda: copy(es.at[jnp.clip(LAST - 1 - s, 0, 1)], late, sems.at[8]).start(),
            )
            choose(
                is_last,
                lambda: copy(tokens, hj, sems.at[9]).start(),
                lambda: copy(hs.at[jnp.clip(other - 1, 0, 1)], hj, sems.at[9]).start(),
            )
            copy(ps.at[other], pj, sems.at[10]).start()

    copy(tokens, h, sems.at[0]).wait()
    copy(tokens, p, sems.at[1]).wait()
    when(s < HALF - 1, lambda: copy(p, ps.at[s if opening else jnp.minimum(s, 2)], sems.at[11]).start())
    arrived(wf, 2)

    def inputs_of(first, partner, mask, g):
        return jnp.concatenate((first[:, lanes(g)], partner[:, lanes(g ^ mask)]), axis=1)

    for g in range(blocks):
        summed = jnp.dot(
            inputs_of(h, p, mask_f, g), factor_matrix(wf, g), preferred_element_type=F32
        )
        hn[:, lanes(g)] = summed.astype(BF)

    if opening:
        copy(cotangent, e, sems.at[6]).wait()
    else:
        copy(ds, d, sems.at[6]).wait()
        copy(r0, mq, sems.at[7]).wait()
        for g in range(blocks):
            moved = mq[:, lanes(g ^ mask_b)].astype(F32)
            e[:, lanes(g)] = (d[:, lanes(g)].astype(F32) + moved).astype(BF)

        @pl.when(s == HALF - 1)
        def _():
            for g in range(blocks):
                pre = hn[:, lanes(g)].astype(F32)
                cdf = 0.5 * (1.0 + lax.erf(pre * SQRT_HALF))
                hn[:, lanes(g)] = (pre * cdf).astype(BF)
                slope = cdf + pre * jnp.exp(-0.5 * pre * pre) * INV_SQRT_TWO_PI
                e[:, lanes(g)] = (e[:, lanes(g)].astype(F32) * slope).astype(BF)

    def send_on():
        when(
            s < 2, lambda: copy(hn, hs.at[jnp.minimum(s, 1)], sems.at[12]).start()
        )
        choose(
            second_next,
            lambda: copy(hn, c1, sems.at[13]).start(),
            lambda: copy(hn, c0, sems.at[13]).start(),
        )

    choose(is_last, lambda: copy(hn, out, sems.at[12]).start(), send_on)
    keeps_grad = False if opening else (s == 1) | (s == 2)
    when(keeps_grad, lambda: copy(e, es.at[jnp.clip(s - 1, 0, 1)], sems.at[14]).start())

    arrived(wb, 4)
    for g in range(blocks):
        both = lax.dot_general(
            e[:, lanes(g)],
            factor_matrix(wb, g),
            (((1,), (1,)), ((), ())),
            preferred_element_type=F32,
        )
        d[:, lanes(g)] = both[:, :128].astype(BF)
        q[:, lanes(g)] = both[:, 128:].astype(BF)
    copy(d, ds, sems.at[15]).start()
    choose(
        second_next,
        lambda: copy(q, c0, sems.at[16]).start(),
        lambda: copy(q, c1, sems.at[16]).start(),
    )

    def share_of(first, partner, mask, grad, slot):
        for g in range(blocks):
            got = weight_share(inputs_of(first, partner, mask, g), grad[:, lanes(g)])
            store_shares(got, core, slot, g, mine_v, theirs_v)

    def store(count, first):
        held = pl.ds(0, count)
        copies = [
            copy(mine_v.at[:, held], mine.at[:, pl.ds(first, count)], sems.at[17]),
            copy(theirs_v.at[:, held], theirs.at[:, pl.ds(first, count)], sems.at[18]),
        ]
        for one in copies:
            one.start()
        for one in copies:
            one.wait()

    def two_shares():
        copy(tokens, late, sems.at[8]).wait()
        copy(tokens, hj, sems.at[9]).wait()
        copy(tokens, pj, sems.at[10]).wait()
        share_of(h, p, mask_f, late, 0)
        share_of(hj, pj, mask_e, e, 1)
        store(2, jnp.clip((s - HALF) * 2, 0, 4))

    def one_share():
        share_of(h, p, mask_f, e, 0)
        store(1, LAST)

    when(late_half, two_shares)
    when(is_half, one_share)
    when((s < 2) | is_last, lambda: copy(hn, out, sems.at[12]).wait())
    choose(is_last, lambda: None, lambda: copy(hn, c0, sems.at[13]).wait())
    when(s < HALF - 1, lambda: copy(p, ps.at[0], sems.at[11]).wait())
    when(keeps_grad, lambda: copy(e, es.at[0], sems.at[14]).wait())
    copy(d, ds, sems.at[15]).wait()
    copy(q, c0, sems.at[16]).wait()


def run_step(opening, info, at, weights, tokens, cotangent, received, state):
    rows, width = tokens.shape
    blocks = width // 128
    act = pltpu.VMEM((rows, width), BF)
    matrix = pltpu.VMEM((8, 2, blocks, 2, 8, 128), BF)
    share = pltpu.VMEM((8, 2, blocks, 2, 8, 128), BF)
    shapes = [jax.ShapeDtypeStruct(part.shape, part.dtype) for part in state]
    first = 10
    return pl.pallas_call(
        partial(step_kernel, opening),
        in_specs=[SMEM, SMEM] + [ANY] * (first + STATE - 2),
        out_specs=[ANY] * len(shapes),
        out_shape=shapes,
        scratch_shapes=[act, act, matrix, matrix, act]
        + [act] * 7
        + [share, share, pltpu.SemaphoreType.DMA((19,))],
        input_output_aliases={first + i: i for i in range(STATE)},
        cost_estimate=pl.CostEstimate(flops=4 * 10**8, bytes_accessed=6 * 10**6, transcendentals=0),
        name="butterfly_step",
    )(info, at, *weights, tokens, cotangent, *received, *state)


def last_kernel(info, direct_ref, moved_ref, out_ref):
    mask = info[0, 0]
    for g in range(direct_ref.shape[1] // 128):
        moved = moved_ref[:, lanes(g ^ mask)].astype(F32)
        out_ref[:, lanes(g)] = (direct_ref[:, lanes(g)].astype(F32) + moved).astype(BF)


def run_last(info, direct, moved):
    whole = pl.BlockSpec(memory_space=pltpu.VMEM)
    return pl.pallas_call(
        last_kernel,
        in_specs=[SMEM, whole, whole],
        out_specs=whole,
        out_shape=jax.ShapeDtypeStruct(direct.shape, direct.dtype),
        name="input_grad_sum",
    )(info, direct, moved)


def allocate(shapes):
    return pl.pallas_call(
        lambda *refs: None, out_specs=[ANY] * len(shapes), out_shape=shapes, name="buffers"
    )()


def shards(tokens, cotangent, weights, strides):
    rows, width = tokens.shape
    block_count = weights.shape[2]
    local_bits = block_count.bit_length() - 1
    fsdp = lax.axis_size("fsdp")
    kinds = 1 + FACTORS - local_bits
    bit = strides - local_bits
    kind = jnp.where(bit < 0, 0, jnp.where(bit == 0, kinds - 1, bit))
    mask = jnp.where(strides < local_bits, 1 << strides, 0)
    core = lax.axis_index("fsdp") & 1

    forward_kind = jnp.append(kind, 0)
    backward_kind = jnp.append(0, kind[::-1])
    low = jnp.minimum(forward_kind, backward_kind)
    high = jnp.maximum(forward_kind, backward_kind)
    plans = pair_plans(kinds)
    numbers = [[0] * kinds for _ in range(kinds)]
    for number, (lo, hi) in enumerate(plans):
        numbers[lo][hi] = number
    index = jnp.asarray(numbers, jnp.int32)[low, high]
    second = forward_kind > backward_kind
    second = jnp.append(second[:FACTORS], True)
    columns = [jnp.append(mask, 0), jnp.append(0, mask[::-1]), second, jnp.full((8,), core)]
    info = jnp.stack([c.astype(jnp.int32) for c in columns], axis=1)

    groups = [list(range(c, fsdp, 2)) for c in range(2)]
    across = partial(
        lax.all_to_all, axis_name="fsdp", split_axis=0, concat_axis=0, axis_index_groups=groups
    )
    twin = [(i, i ^ 1) for i in range(fsdp)]
    shard = weights.transpose(0, 2, 3, 1, 4)

    def copies(part):
        return jnp.broadcast_to(part[None], (fsdp // 2,) + part.shape)

    def with_pair(own):
        return own, lax.ppermute(own, "fsdp", twin)

    ends = across(copies(jnp.stack((shard[0], shard[LAST]))))
    middle = copies(shard[1:LAST])
    first = exchange_one(tokens, kind[0], kinds)
    ends, first = lax.optimization_barrier((ends, first))
    middle, ends = lax.optimization_barrier((middle, ends))
    middle = across(middle)
    ends = with_pair(ends)

    act = jax.ShapeDtypeStruct((rows, width), BF)
    share = jax.ShapeDtypeStruct((8, FACTORS, block_count, 2, 8, 128), BF)
    stack = lambda count: jax.ShapeDtypeStruct((count, rows, width), BF)
    state = allocate([stack(2), stack(3), stack(2), act, act, act, share, share, act])
    at = jnp.zeros((1,), jnp.int32)
    state = run_step(True, info, at, ends + ends, tokens, cotangent, (first, first), state)
    packed = jnp.sum(index << (4 * jnp.arange(8)), dtype=jnp.int32)

    def pair_exchange(step, held):
        return exchange_two(held[4], held[5], (packed >> (4 * step)) & 15, kinds)

    def finish(step, received, held, matrices):
        args = (info, step[None], matrices + ends, tokens, cotangent, received, held)
        return tuple(run_step(False, *args))

    received = pair_exchange(1, state)
    middle, received = lax.optimization_barrier((middle, received))
    middle = with_pair(middle)
    state = finish(jnp.int32(1), received, state, middle)

    def body(step, held):
        return finish(step, pair_exchange(step, held), held, middle)

    state = lax.fori_loop(2, FACTORS, body, state)
    direct, crossed, mine, theirs, output = state[3], state[4], state[6], state[7], state[8]

    arrived = lax.ppermute(theirs, "fsdp", twin)
    chip_sum = (mine.astype(F32) + arrived.astype(F32)).astype(BF)
    parts = across(chip_sum)
    moved = exchange_one(crossed, kind[0], kinds)
    parts, _ = lax.optimization_barrier((parts, moved))
    input_grad = run_last(info, direct, moved)
    total = jnp.sum(parts.astype(F32), axis=0)
    total = jnp.stack([total[SLOTS[f]] for f in range(FACTORS)])
    weight_grad = total.transpose(0, 3, 1, 2, 4)
    return (output, input_grad, weight_grad)


def solution(mesh):
    in_specs = (P("fsdp", "hid"), P("fsdp", "hid"), P(None, "fsdp", "hid", None, None), P())
    out_specs = (P("fsdp", "hid"), P("fsdp", "hid"), P(None, "fsdp", "hid", None, None))
    return jax.shard_map(shards, mesh=mesh, in_specs=in_specs, out_specs=out_specs, check_vma=False)
```

```python
from functools import partial

import jax
import jax.numpy as jnp
from jax import lax
from jax.experimental import pallas as pl
from jax.experimental.pallas import tpu as pltpu
from jax.sharding import PartitionSpec as P

HALF = 4
FACTORS = 7
LAST = FACTORS - 1
SQRT_HALF = 0.7071067811865476
INV_SQRT_TWO_PI = 0.3989422804014327
BF = jnp.bfloat16
F32 = jnp.float32
SLOTS = {3: 6, 4: 0, 2: 1, 5: 2, 1: 3, 6: 4, 0: 5}
ANY = pl.BlockSpec(memory_space=pl.ANY)
SMEM = pl.BlockSpec(memory_space=pltpu.SMEM)
STATE = 9


def swapped(block, kind):
    if kind == 0:
        return block
    count = lax.axis_size("hid")
    distance = kind % (count.bit_length() - 1)
    return lax.ppermute(block, "hid", [(low, low ^ (1 << distance)) for low in range(count)])


def exchange_one(block, kind, kinds):
    return lax.switch(kind, [partial(swapped, kind=k) for k in range(kinds)], block)


def pair_plans(kinds):
    return [(0, 0)] + [(lo, hi) for lo in range(kinds) for hi in range(lo + 1, kinds)]


def exchange_two(first, second, index, kinds):
    def branch(plan, a, b):
        return swapped(a, plan[0]), swapped(b, plan[1])

    return lax.switch(index, [partial(branch, plan) for plan in pair_plans(kinds)], first, second)


def lanes(g):
    return pl.ds(pl.multiple_of(g * 128, 128), 128)


def factor_matrix(ref, g):
    rows = ref[:, :, g].astype(F32)
    own = rows[:, :, 0].reshape(128, 128)
    pair = rows[:, :, 1].reshape(128, 128)
    return jnp.concatenate((own, pair), axis=0).astype(BF)


def store_shares(grad, core, slot, g, mine_ref, theirs_ref):
    halves = grad.reshape(2, 8, 2, 8, 128)
    for side in range(2):
        even, odd = halves[side, :, 0], halves[side, :, 1]
        mine_ref[:, slot, g, side] = jnp.where(core == 0, even, odd).astype(BF)
        theirs_ref[:, slot, g, side] = jnp.where(core == 0, odd, even).astype(BF)


def weight_share(inputs, grad):
    return lax.dot_general(inputs, grad, (((0,), (0,)), ((), ())), preferred_element_type=F32)


def when(flag, act):
    if flag is True:
        act()
    elif flag is not False:
        pl.when(flag)(act)


def choose(flag, yes, no):
    when(flag, yes)
    when((not flag) if isinstance(flag, bool) else jnp.logical_not(flag), no)


def step_kernel(opening, *refs):
    info, at, wa, wa_pair, wz, wz_pair, tokens, cotangent, r0, r1 = refs[:10]
    refs = refs[10 + STATE :]
    hs, ps, es, ds, c0, c1, mine, theirs, out = refs[:STATE]
    h, p, wf, wb, d, mq, e, hn, q, hj, pj, late, mine_v, theirs_v, sems = refs[STATE:]
    blocks = h.shape[1] // 128
    s = 0 if opening else at[0]
    is_last = False if opening else s == LAST
    is_half = False if opening else s == HALF - 1
    late_half = False if opening else s >= HALF
    other = LAST - s
    mask_f, mask_b = info[s, 0], info[s, 1]
    second, second_next = info[s, 2] == 1, info[s + 1, 2] == 1
    mask_e = info[other, 0]
    core = info[0, 3]
    copy = pltpu.make_async_copy

    def fetch(own, pair, factor, held, sem):
        copy(own.at[:, factor], held.at[:, core], sems.at[sem]).start()
        copy(pair.at[:, factor], held.at[:, 1 - core], sems.at[sem + 1]).start()

    def arrived(held, sem):
        copy(wz.at[:, 0], held.at[:, 0], sems.at[sem]).wait()
        copy(wz.at[:, 0], held.at[:, 0], sems.at[sem + 1]).wait()

    if opening:
        copy(tokens, h, sems.at[0]).start()
        fetch(wz, wz_pair, 0, wf, 2)
    else:
        choose(
            second,
            lambda: copy(c1, h, sems.at[0]).start(),
            lambda: copy(c0, h, sems.at[0]).start(),
        )
    choose(
        second,
        lambda: copy(r1, p, sems.at[1]).start(),
        lambda: copy(r0, p, sems.at[1]).start(),
    )
    if opening:
        fetch(wz, wz_pair, 1, wb, 4)
        copy(cotangent, e, sems.at[6]).start()
    else:

        def fetch_end():
            fetch(wz, wz_pair, 1, wf, 2)
            fetch(wz, wz_pair, 0, wb, 4)

        def fetch_middle():
            fetch(wa, wa_pair, s - 1, wf, 2)
            fetch(wa, wa_pair, other - 1, wb, 4)

        choose(is_last, fetch_end, fetch_middle)
        copy(ds, d, sems.at[6]).start()
        choose(
            second,
            lambda: copy(r0, mq, sems.at[7]).start(),
            lambda: copy(r1, mq, sems.at[7]).start(),
        )

        @pl.when(s >= HALF)
        def _():
            choose(
                is_last,
                lambda: copy(cotangent, late, sems.at[8]).start(),
                lambda: copy(es.at[jnp.clip(LAST - 1 - s, 0, 1)], late, sems.at[8]).start(),
            )
            choose(
                is_last,
                lambda: copy(tokens, hj, sems.at[9]).start(),
                lambda: copy(hs.at[jnp.clip(other - 1, 0, 1)], hj, sems.at[9]).start(),
            )
            copy(ps.at[other], pj, sems.at[10]).start()

    copy(tokens, h, sems.at[0]).wait()
    copy(tokens, p, sems.at[1]).wait()
    when(s < HALF - 1, lambda: copy(p, ps.at[s if opening else jnp.minimum(s, 2)], sems.at[11]).start())
    arrived(wf, 2)

    def inputs_of(first, partner, mask, g):
        return jnp.concatenate((first[:, lanes(g)], partner[:, lanes(g ^ mask)]), axis=1)

    for g in range(blocks):
        summed = jnp.dot(
            inputs_of(h, p, mask_f, g), factor_matrix(wf, g), preferred_element_type=F32
        )
        hn[:, lanes(g)] = summed.astype(BF)

    if opening:
        copy(cotangent, e, sems.at[6]).wait()
    else:
        copy(ds, d, sems.at[6]).wait()
        copy(r0, mq, sems.at[7]).wait()
        for g in range(blocks):
            moved = mq[:, lanes(g ^ mask_b)].astype(F32)
            e[:, lanes(g)] = (d[:, lanes(g)].astype(F32) + moved).astype(BF)

        @pl.when(s == HALF - 1)
        def _():
            for g in range(blocks):
                pre = hn[:, lanes(g)].astype(F32)
                cdf = 0.5 * (1.0 + lax.erf(pre * SQRT_HALF))
                hn[:, lanes(g)] = (pre * cdf).astype(BF)
                slope = cdf + pre * jnp.exp(-0.5 * pre * pre) * INV_SQRT_TWO_PI
                e[:, lanes(g)] = (e[:, lanes(g)].astype(F32) * slope).astype(BF)

    def send_on():
        when(
            s < 2, lambda: copy(hn, hs.at[jnp.minimum(s, 1)], sems.at[12]).start()
        )
        choose(
            second_next,
            lambda: copy(hn, c1, sems.at[13]).start(),
            lambda: copy(hn, c0, sems.at[13]).start(),
        )

    choose(is_last, lambda: copy(hn, out, sems.at[12]).start(), send_on)
    keeps_grad = False if opening else (s == 1) | (s == 2)
    when(keeps_grad, lambda: copy(e, es.at[jnp.clip(s - 1, 0, 1)], sems.at[14]).start())

    def half_of(part, half):
        return part.at[:, half * blocks * 64 : (half + 1) * blocks * 64]

    def send_half(half):
        part = half_of(q, half)
        choose(
            second_next,
            lambda: copy(part, half_of(c0, half), sems.at[16 + 4 * half]).start(),
            lambda: copy(part, half_of(c1, half), sems.at[16 + 4 * half]).start(),
        )
        copy(half_of(d, half), half_of(ds, half), sems.at[15 + 4 * half]).start()

    arrived(wb, 4)
    for g in range(blocks):
        both = lax.dot_general(
            e[:, lanes(g)],
            factor_matrix(wb, g),
            (((1,), (1,)), ((), ())),
            preferred_element_type=F32,
        )
        d[:, lanes(g)] = both[:, :128].astype(BF)
        q[:, lanes(g)] = both[:, 128:].astype(BF)
        if (g + 1) % (blocks // 2) == 0:
            send_half((g + 1) // (blocks // 2) - 1)

    def share_of(first, partner, mask, grad, slot):
        for g in range(blocks):
            got = weight_share(inputs_of(first, partner, mask, g), grad[:, lanes(g)])
            store_shares(got, core, slot, g, mine_v, theirs_v)

    def store(count, first):
        held = pl.ds(0, count)
        copies = [
            copy(mine_v.at[:, held], mine.at[:, pl.ds(first, count)], sems.at[17]),
            copy(theirs_v.at[:, held], theirs.at[:, pl.ds(first, count)], sems.at[18]),
        ]
        for one in copies:
            one.start()
        for one in copies:
            one.wait()

    def two_shares():
        copy(tokens, late, sems.at[8]).wait()
        copy(tokens, hj, sems.at[9]).wait()
        copy(tokens, pj, sems.at[10]).wait()
        share_of(h, p, mask_f, late, 0)
        share_of(hj, pj, mask_e, e, 1)
        store(2, jnp.clip((s - HALF) * 2, 0, 4))

    def one_share():
        share_of(h, p, mask_f, e, 0)
        store(1, LAST)

    when(late_half, two_shares)
    when(is_half, one_share)
    when((s < 2) | is_last, lambda: copy(hn, out, sems.at[12]).wait())
    choose(is_last, lambda: None, lambda: copy(hn, c0, sems.at[13]).wait())
    when(s < HALF - 1, lambda: copy(p, ps.at[0], sems.at[11]).wait())
    when(keeps_grad, lambda: copy(e, es.at[0], sems.at[14]).wait())
    for half in range(2):
        copy(half_of(d, half), half_of(ds, half), sems.at[15 + 4 * half]).wait()
        copy(half_of(q, half), half_of(c0, half), sems.at[16 + 4 * half]).wait()


def run_step(opening, info, at, weights, tokens, cotangent, received, state):
    rows, width = tokens.shape
    blocks = width // 128
    act = pltpu.VMEM((rows, width), BF)
    matrix = pltpu.VMEM((8, 2, blocks, 2, 8, 128), BF)
    share = pltpu.VMEM((8, 2, blocks, 2, 8, 128), BF)
    shapes = [jax.ShapeDtypeStruct(part.shape, part.dtype) for part in state]
    first = 10
    return pl.pallas_call(
        partial(step_kernel, opening),
        in_specs=[SMEM, SMEM] + [ANY] * (first + STATE - 2),
        out_specs=[ANY] * len(shapes),
        out_shape=shapes,
        scratch_shapes=[act, act, matrix, matrix, act]
        + [act] * 7
        + [share, share, pltpu.SemaphoreType.DMA((21,))],
        input_output_aliases={first + i: i for i in range(STATE)},
        cost_estimate=pl.CostEstimate(flops=4 * 10**8, bytes_accessed=6 * 10**6, transcendentals=0),
        name="butterfly_step",
    )(info, at, *weights, tokens, cotangent, *received, *state)


def last_kernel(info, direct_ref, moved_ref, out_ref):
    mask = info[0, 0]
    for g in range(direct_ref.shape[1] // 128):
        moved = moved_ref[:, lanes(g ^ mask)].astype(F32)
        out_ref[:, lanes(g)] = (direct_ref[:, lanes(g)].astype(F32) + moved).astype(BF)


def run_last(info, direct, moved):
    whole = pl.BlockSpec(memory_space=pltpu.VMEM)
    return pl.pallas_call(
        last_kernel,
        in_specs=[SMEM, whole, whole],
        out_specs=whole,
        out_shape=jax.ShapeDtypeStruct(direct.shape, direct.dtype),
        name="input_grad_sum",
    )(info, direct, moved)


def allocate(shapes):
    return pl.pallas_call(
        lambda *refs: None, out_specs=[ANY] * len(shapes), out_shape=shapes, name="buffers"
    )()


def shards(tokens, cotangent, weights, strides):
    rows, width = tokens.shape
    block_count = weights.shape[2]
    local_bits = block_count.bit_length() - 1
    fsdp = lax.axis_size("fsdp")
    kinds = 1 + FACTORS - local_bits
    bit = strides - local_bits
    kind = jnp.where(bit < 0, 0, jnp.where(bit == 0, kinds - 1, bit))
    mask = jnp.where(strides < local_bits, 1 << strides, 0)
    core = lax.axis_index("fsdp") & 1

    forward_kind = jnp.append(kind, 0)
    backward_kind = jnp.append(0, kind[::-1])
    low = jnp.minimum(forward_kind, backward_kind)
    high = jnp.maximum(forward_kind, backward_kind)
    plans = pair_plans(kinds)
    numbers = [[0] * kinds for _ in range(kinds)]
    for number, (lo, hi) in enumerate(plans):
        numbers[lo][hi] = number
    index = jnp.asarray(numbers, jnp.int32)[low, high]
    second = forward_kind > backward_kind
    second = jnp.append(second[:FACTORS], True)
    columns = [jnp.append(mask, 0), jnp.append(0, mask[::-1]), second, jnp.full((8,), core)]
    info = jnp.stack([c.astype(jnp.int32) for c in columns], axis=1)

    groups = [list(range(c, fsdp, 2)) for c in range(2)]
    across = partial(
        lax.all_to_all, axis_name="fsdp", split_axis=0, concat_axis=0, axis_index_groups=groups
    )
    twin = [(i, i ^ 1) for i in range(fsdp)]
    shard = weights.transpose(0, 2, 3, 1, 4)

    def copies(part):
        return jnp.broadcast_to(part[None], (fsdp // 2,) + part.shape)

    def with_pair(own):
        return own, lax.ppermute(own, "fsdp", twin)

    ends = across(copies(jnp.stack((shard[0], shard[LAST]))))
    middle = copies(shard[1:LAST])
    first = exchange_one(tokens, kind[0], kinds)
    ends, first = lax.optimization_barrier((ends, first))
    middle, ends = lax.optimization_barrier((middle, ends))
    middle = across(middle)
    ends = with_pair(ends)

    act = jax.ShapeDtypeStruct((rows, width), BF)
    share = jax.ShapeDtypeStruct((8, FACTORS, block_count, 2, 8, 128), BF)
    stack = lambda count: jax.ShapeDtypeStruct((count, rows, width), BF)
    state = allocate([stack(2), stack(3), stack(2), act, act, act, share, share, act])
    at = jnp.zeros((1,), jnp.int32)
    state = run_step(True, info, at, ends + ends, tokens, cotangent, (first, first), state)
    packed = jnp.sum(index << (4 * jnp.arange(8)), dtype=jnp.int32)

    def pair_exchange(step, held):
        return exchange_two(held[4], held[5], (packed >> (4 * step)) & 15, kinds)

    def finish(step, received, held, matrices):
        args = (info, step[None], matrices + ends, tokens, cotangent, received, held)
        return tuple(run_step(False, *args))

    received = pair_exchange(1, state)
    middle, received = lax.optimization_barrier((middle, received))
    middle = with_pair(middle)
    state = finish(jnp.int32(1), received, state, middle)

    def body(step, held):
        return finish(step, pair_exchange(step, held), held, middle)

    state = lax.fori_loop(2, FACTORS, body, state)
    direct, crossed, mine, theirs, output = state[3], state[4], state[6], state[7], state[8]

    arrived = lax.ppermute(theirs, "fsdp", twin)
    chip_sum = (mine.astype(F32) + arrived.astype(F32)).astype(BF)
    parts = across(chip_sum)
    moved = exchange_one(crossed, kind[0], kinds)
    parts, _ = lax.optimization_barrier((parts, moved))
    input_grad = run_last(info, direct, moved)
    total = jnp.sum(parts.astype(F32), axis=0)
    total = jnp.stack([total[SLOTS[f]] for f in range(FACTORS)])
    weight_grad = total.transpose(0, 3, 1, 2, 4)
    return (output, input_grad, weight_grad)


def solution(mesh):
    in_specs = (P("fsdp", "hid"), P("fsdp", "hid"), P(None, "fsdp", "hid", None, None), P())
    out_specs = (P("fsdp", "hid"), P("fsdp", "hid"), P(None, "fsdp", "hid", None, None))
    return jax.shard_map(shards, mesh=mesh, in_specs=in_specs, out_specs=out_specs, check_vma=False)
```
